256 devices in a mesh: row: 128 (over z, y, x), col: 2 (over core).
Axes of the slice: x: 4, y: 4, z: 8, core: 2. Of those that a mesh axis runs over, the one named last changes fastest.
Arguments:
- panel_column: float32 [2, 32768, 256], P(None, 'row'), may hold values from -9 to 201, as said below
- trailing: float32 [2, 32768, 1, 512], P(None, 'row', None, 'col'), may hold values from -6 to 262
Outputs:
- panel_factor: float32 [2, 32768, 256], P(None, 'row')
- updated: float32 [2, 32768, 1, 512], P(None, 'row', None, 'col')
- next_panel: float32 [2, 32768, 256], P(None, 'row', 'col')
The draws below stay inside these ranges and needn't reach their ends.
Inputs may be any that keep to these rules, and one draw needn't show every extreme that they name: The first 256 rows of panel_column form a symmetric positive definite block; the rows 256 to 512 of the first 256 columns of updated form a block whose symmetric part is positive definite.
All inputs are finite; a program needn't handle non-finite values.
Results may differ from the reference program's by a relative error of at most 0.00005.
Values sent between devices are 32-bit elements; how exact they have to be, the bound alone decides.
No kernel may reach another device: no remote copies, remote signals or barrier semaphores. Data moves between devices by JAX's collectives and lax.ppermute only.
A program may use at most 64 MiB of HBM per device.

```python
import jax
import jax.numpy as jnp
from jax import lax

PANEL = 256
ORDER = 65536
COL_SLOTS = 1
SLOTS = 2
SLAB = 512


def draw_panel_column(key, part):
    keys = jax.random.split(jax.random.fold_in(key, 11), 2)
    noise = jnp.clip(jax.random.normal(keys[0], (ORDER, PANEL), jnp.float32), -6.0, 6.0)
    head_block = noise[:PANEL]
    head_block = (head_block + head_block.T) * 0.7071
    spread = jax.random.uniform(keys[1], (PANEL,), jnp.float32, 96.0, 192.0)
    head_block = head_block + jnp.diag(spread)
    whole = jnp.concatenate([head_block, noise[PANEL:]], 0)
    return whole.reshape(SLOTS, ORDER // SLOTS, PANEL)


def draw_trailing(key, part):
    keys = jax.random.split(jax.random.fold_in(key, 23), 2)
    noise = jnp.clip(jax.random.normal(keys[0], (ORDER, SLAB), jnp.float32), -6.0, 6.0)
    spread = jax.random.uniform(keys[1], (SLAB,), jnp.float32, 128.0, 256.0)
    places = jnp.arange(SLAB)
    noise = noise.at[PANEL + places, places].add(spread)
    return noise.reshape(SLOTS, ORDER // SLOTS, COL_SLOTS, SLAB // COL_SLOTS)


def setup_inputs(seed: int = 0) -> dict:
    key_list = jax.random.split(jax.random.key(seed), 3)
    return {
        "panel_column": draw_panel_column(jax.random.fold_in(key_list[2], 71), 0),
        "trailing": draw_trailing(jax.random.fold_in(key_list[2], 71), 0),
    }


def lower_factor(square):
    return jnp.linalg.cholesky(0.5 * (square + square.T))

def right_solve(factor, rows_in):
    return jax.scipy.linalg.solve_triangular(factor, rows_in.T, lower=True).T

def reference(panel_column, trailing):
    whole = panel_column.reshape(ORDER, PANEL)
    slab_all = trailing.reshape(ORDER, SLAB)
    factor = lower_factor(whole[:PANEL])
    below = right_solve(factor, whole[PANEL:])
    panel_factor = jnp.concatenate([factor, below], 0).reshape(panel_column.shape)
    zero_block = jnp.zeros((PANEL, PANEL), jnp.float32)
    carried = jnp.concatenate([zero_block, below], 0)
    change = jnp.dot(carried.astype(jnp.float32), below[:SLAB].T.astype(jnp.float32), precision=lax.Precision.HIGHEST, preferred_element_type=jnp.float32)
    updated_all = slab_all - change
    lead_column = updated_all[:, :PANEL]
    factor_next = lower_factor(lead_column[PANEL:2 * PANEL])
    below_next = right_solve(factor_next, lead_column[2 * PANEL:])
    next_all = jnp.concatenate([zero_block, factor_next, below_next], 0).reshape(panel_column.shape)
    return (panel_factor, updated_all.reshape(trailing.shape), next_all)
```

```python
import functools

import jax
import jax.numpy as jnp
from jax import lax
from jax.experimental import pallas as pl
from jax.experimental.pallas import tpu as pltpu
from jax.sharding import Mesh, PartitionSpec as P

N = 256
NB = 16
STEPS = N // NB


def dot_nt(a, b):
    return lax.dot_general(
        a, b, (((1,), (1,)), ((), ())),
        precision=lax.Precision.HIGHEST, preferred_element_type=jnp.float32,
    )


def dot_nn(a, b):
    return lax.dot_general(
        a, b, (((1,), (0,)), ((), ())),
        precision=lax.Precision.HIGHEST, preferred_element_type=jnp.float32,
    )


def factor_inverse(w, spl, xb, zb, tt):
    lane = lax.broadcasted_iota(jnp.int32, (NB, N), 1)
    sub = lax.broadcasted_iota(jnp.int32, (NB, N), 0)
    lane_all = lax.broadcasted_iota(jnp.int32, (N, N), 1)
    row_all = lax.broadcasted_iota(jnp.int32, (N, N), 0)
    zb[...] = jnp.zeros((NB, N), jnp.float32)
    tt[...] = jnp.zeros((N, NB), jnp.float32)

    def step(b, carry):
        r0 = pl.multiple_of(b * NB, NB)
        rows = w[pl.ds(r0, NB), :]
        half = jnp.where(b < STEPS // 2, rows[:, :128], rows[:, 128:])
        base = lax.rem(r0, 128)
        for j in range(NB):
            idx = jnp.full((NB, 128), base + j, jnp.int32)
            spl[j] = jnp.take_along_axis(half, idx, axis=1)
        in_block = (lane >= r0) & (lane < r0 + NB)
        unit = jnp.where(lane - r0 == sub, 1.0, 0.0)
        xb[...] = jnp.where(in_block, unit, rows)
        z_old = zb[...]
        late = dot_nn(tt[...], z_old)
        old = w[...]
        gone = (lane_all >= r0 - NB) & (lane_all < r0)
        w[...] = jnp.where(row_all >= r0 + NB, jnp.where(gone, 0.0, old) - late, old)
        s = [[spl[j, i:i + 1, :] for j in range(i + 1)] for i in range(NB)]
        x = [[xb[i:i + 1, 128 * h:128 * h + 128] for h in range(2)] for i in range(NB)]
        for k in range(NB):
            r = lax.rsqrt(s[k][k])
            y = [x[k][h] * r for h in range(2)]
            for h in range(2):
                zb[k:k + 1, 128 * h:128 * h + 128] = y[h]
            col = [None] * NB
            for i in range(k + 1, NB):
                col[i] = s[i][k] * r
                for j in range(k + 1, i + 1):
                    s[i][j] = s[i][j] - col[i] * col[j]
                for h in range(2):
                    x[i][h] = x[i][h] - col[i] * y[h]
        z = zb[...]
        tt[...] = jnp.where(lane >= r0 + NB, z, 0.0).T
        n0 = pl.multiple_of(jnp.minimum(r0 + NB, N - NB), NB)
        near = w[pl.ds(n0, NB), :]
        near = jnp.where(in_block, 0.0, near) - dot_nn(tt[pl.ds(n0, NB), :], z)
        w[pl.ds(n0, NB), :] = near
        w[pl.ds(r0, NB), :] = z
        return carry

    lax.fori_loop(0, STEPS, step, 0)
    return jnp.where(lane_all <= row_all, w[...], 0.0)


def kernel(flags, mine, other, panel, trail, trail_other, pf, up, nx, w, spl, xb, zb, tt):
    row, core = flags[0], flags[1]
    is0 = core == 0
    lane_all = lax.broadcasted_iota(jnp.int32, (N, N), 1)
    row_all = lax.broadcasted_iota(jnp.int32, (N, N), 0)
    low = lane_all <= row_all

    def both(lo, hi):
        m, o = mine[:, lo:hi, :], other[:, lo:hi, :]
        size = 16 * (hi - lo)
        return jnp.where(is0, m, o).reshape(size, N), jnp.where(is0, o, m).reshape(size, N)

    head = jnp.concatenate(both(0, 8), 0)
    corner, block1 = both(8, 24)
    block2 = jnp.concatenate(both(24, 32), 0)
    head = 0.5 * (head + head.T)
    w[...] = head
    inv1 = factor_inverse(w, spl, xb, zb, tt)
    below1 = dot_nt(block1, inv1)
    below_own = dot_nt(jnp.where(is0, block1, block2), inv1)
    corner = corner - dot_nt(below1, below1)
    corner = 0.5 * (corner + corner.T)
    w[...] = corner
    for slot in range(2):
        rows = pl.ds(slot * N, N)
        first = (row == 0) if slot == 0 else False
        solved = dot_nt(panel[rows, :], inv1)
        carried = solved
        if slot == 0:
            solved = jnp.where(first & ~low, 0.0, solved)
            carried = jnp.where(first, 0.0, solved)
        pf[rows, :] = solved
        up[rows, :] = trail[rows, :] - dot_nt(carried, below_own)
        lead = jnp.where(is0, trail[rows, :], trail_other[rows, :]) - dot_nt(carried, below1)
        if slot == 0:
            lead = jnp.where(row == 1, corner, lead)
        trail_other[rows, :] = lead
    inv2 = factor_inverse(w, spl, xb, zb, tt)
    half = jnp.where(is0, inv2[:128], inv2[128:])
    low_half = lane_all[:, :128] + core * 128 <= row_all[:, :128]
    for slot in range(2):
        rows = pl.ds(slot * N, N)
        solved = dot_nt(trail_other[rows, :], half)
        if slot == 0:
            solved = jnp.where((row == 0) | ((row == 1) & ~low_half), 0.0, solved)
        nx[rows, :] = solved


def local_part(flags, mine, other, panel, trail, trail_other):
    vmem = pl.BlockSpec(memory_space=pltpu.VMEM)
    f32 = jnp.float32
    return pl.pallas_call(
        kernel,
        out_shape=[
            jax.ShapeDtypeStruct((512, N), f32),
            jax.ShapeDtypeStruct((512, N), f32),
            jax.ShapeDtypeStruct((512, 128), f32),
        ],
        in_specs=[pl.BlockSpec(memory_space=pltpu.SMEM)] + [vmem] * 5,
        out_specs=[vmem] * 3,
        scratch_shapes=[
            pltpu.VMEM((N, N), f32),
            pltpu.VMEM((NB, NB, 128), f32),
            pltpu.VMEM((NB, N), f32),
            pltpu.VMEM((NB, N), f32),
            pltpu.VMEM((N, NB), f32),
        ],
        compiler_params=pltpu.CompilerParams(vmem_limit_bytes=40 << 20),
        name="panel_step",
    )(flags, mine, other, panel, trail, trail_other)


def on_device(panel, trail):
    plane = ("y", "x")
    z = lax.axis_index("z")
    member = lax.axis_index(plane)
    core = lax.axis_index("core")
    row = z * lax.axis_size(plane) + member
    trail_other = lax.ppermute(trail.reshape(512, N), "core", [(0, 1), (1, 0)])
    block = panel[0]
    part = lax.dynamic_slice_in_dim(block, core * 128, 128, 0).reshape(16, 8, N)
    part = jnp.concatenate([part, jnp.zeros_like(part)], 1)
    full = jnp.where(core == 0, trail[0, :, 0, :], block).reshape(16, 16, N)
    sent = jnp.where(row == 1, full, part)
    got = lax.all_to_all(sent, plane, 0, 0)
    piece = jnp.concatenate([got[0, :8], got[1], got[2, :8]], 0)
    piece = jnp.where(z == 0, piece, 0.0)
    size = lax.axis_size("z")
    reach = 1
    while reach < size:
        piece = piece + lax.ppermute(piece, "z", [(i, i + reach) for i in range(reach)])
        reach *= 2
    mine = lax.all_to_all(jnp.broadcast_to(piece[None], (16, 32, N)), plane, 0, 0)
    other = lax.ppermute(mine, "core", [(0, 1), (1, 0)])
    flags = jnp.stack([row, core]).astype(jnp.int32)
    pf, up, nx = local_part(
        flags, mine, other, panel.reshape(512, N), trail.reshape(512, N), trail_other
    )
    return pf.reshape(2, N, N), up.reshape(2, N, 1, N), nx.reshape(2, N, 128)


def solution(mesh):
    grid = Mesh(mesh.devices.reshape(8, 4, 4, 2), ("z", "y", "x", "core"))
    rows = ("z", "y", "x")
    return jax.shard_map(
        on_device,
        mesh=grid,
        in_specs=(P(None, rows, None), P(None, rows, None, "core")),
        out_specs=(P(None, rows, None), P(None, rows, None, "core"), P(None, rows, "core")),
        check_vma=False,
    )
```

```python
import functools

import jax
import jax.numpy as jnp
from jax import lax
from jax.experimental import pallas as pl
from jax.experimental.pallas import tpu as pltpu
from jax.sharding import Mesh, PartitionSpec as P

N = 256
NB = 16
STEPS = N // NB
Z_STEPS = (
    [(0, 1)],
    [(0, 7), (1, 2)],
    [(0, 5), (1, 4), (2, 3), (7, 6)],
)


def dot_nt(a, b):
    return lax.dot_general(
        a, b, (((1,), (1,)), ((), ())),
        precision=lax.Precision.HIGHEST, preferred_element_type=jnp.float32,
    )


def split(a):
    high = a.astype(jnp.bfloat16)
    return high, (a - high.astype(jnp.float32)).astype(jnp.bfloat16)


def dot_nt3(a, b):
    a_hi, a_lo = split(a)
    b_hi, b_lo = b

    def part(u, v):
        return lax.dot_general(u, v, (((1,), (1,)), ((), ())), preferred_element_type=jnp.float32)

    return part(a_hi, b_hi) + (part(a_hi, b_lo) + part(a_lo, b_hi))


def dot_nn(a, b):
    return lax.dot_general(
        a, b, (((1,), (0,)), ((), ())),
        precision=lax.Precision.HIGHEST, preferred_element_type=jnp.float32,
    )


def spread_row(ref, i, h):
    return jnp.broadcast_to(ref[i:i + 1, 128 * h:128 * h + 128], (8, 128))


def factor_inverse(w, inv, near, spl, low, mid, xb, zb, tt):
    lane = lax.broadcasted_iota(jnp.int32, (NB, N), 1)
    sub = lax.broadcasted_iota(jnp.int32, (NB, N), 0)
    zb[...] = jnp.zeros((NB, N), jnp.float32)
    near[...] = w[0:NB, :]

    def step(b, carry, top):
        r0 = pl.multiple_of(b * NB, NB)
        n0 = pl.multiple_of(jnp.minimum(r0 + NB, N - NB), NB)
        lo = 128 * top
        base = r0 - lo
        rows = near[...]
        half = rows[:, lo:lo + 128]

        def column(tile, j):
            idx = jnp.full((8, 128), base + j, jnp.int32)
            return jnp.take_along_axis(tile, idx, axis=1)

        for j in range(8):
            spl[8 * j:8 * j + 8, :] = column(half[:8], j)
        v = [[column(half[8:], j)] for j in range(8)]
        d = [column(half[8:], 8 + j) for j in range(8)]
        in_block = (lane >= r0) & (lane < r0 + NB)
        xb[...] = jnp.where(in_block, jnp.where(lane - r0 == sub, 1.0, 0.0), rows)
        z_old = zb[...]
        tt[lo:, :] = jnp.where(lane[:, lo:] >= r0 + NB, z_old[:, lo:], 0.0).T
        gone = (lane >= r0 - NB) & (lane < r0)
        nxt = jnp.where(gone, 0.0, w[pl.ds(n0, NB), :]) - dot_nn(tt[pl.ds(n0, NB), :], z_old)
        for j in range(8):
            v[j] += [column(nxt[:8, lo:lo + 128], j), column(nxt[8:, lo:lo + 128], j)]
        c = [[column(nxt[8 * n:8 * n + 8, lo:lo + 128], 8 + j) for n in range(2)] for j in range(8)]
        nxt = jnp.where(in_block, 0.0, nxt)
        acc = [[nxt[8 * n:8 * n + 8, 128 * h:128 * h + 128] for h in range(2)] for n in range(2)]
        lane_r = lax.broadcasted_iota(jnp.int32, (N - lo, N), 1)
        row_r = lax.broadcasted_iota(jnp.int32, (N - lo, N), 0) + lo
        old = w[lo:, :]
        gone_r = (lane_r >= r0 - NB) & (lane_r < r0)
        w[lo:, :] = jnp.where(
            row_r >= r0 + NB, jnp.where(gone_r, 0.0, old) - dot_nn(tt[lo:, :], z_old), old
        )
        y_all = []
        for g in range(2):
            if g == 0:
                s = [[spread_row(spl, 8 * j + i, 0) for j in range(i + 1)] for i in range(8)]
            else:
                for j in range(8):
                    mid[8 * j:8 * j + 8, :] = d[j]
                s = [[spread_row(mid, 8 * j + i, 0) for j in range(i + 1)] for i in range(8)]
                v = c
            x = [[spread_row(xb, 8 * g + i, h) for h in range(2)] for i in range(8)]
            if g == 1:
                for k in range(8):
                    for i in range(8):
                        for h in range(2):
                            x[i][h] = x[i][h] - cross[k][i] * y_all[k][h]
            cross = []
            for k in range(8):
                r = lax.rsqrt(s[k][k])
                y = [x[k][h] * r for h in range(2)]
                y_all.append(y)
                for h in range(2):
                    zb[8 * g + k:8 * g + k + 1, 128 * h:128 * h + 128] = y[h][:1]
                col = [None] * 8
                for i in range(k + 1, 8):
                    col[i] = s[i][k] * r
                    for j in range(k + 1, i + 1):
                        s[i][j] = s[i][j] - col[i] * col[j]
                    for h in range(2):
                        x[i][h] = x[i][h] - col[i] * y[h]
                v[k] = [t * r for t in v[k]]
                for j in range(k + 1, 8):
                    v[j] = [t - u * col[j] for t, u in zip(v[j], v[k])]
                below = v[k]
                if g == 0:
                    low[8 * k:8 * k + 8, :] = v[k][0]
                    cross.append([spread_row(low, 8 * k + i, 0) for i in range(8)])
                    below = v[k][1:]
                    for j in range(8):
                        d[j] = d[j] - v[k][0] * cross[k][j]
                        c[j] = [t - u * cross[k][j] for t, u in zip(c[j], below)]
                for n in range(2):
                    for h in range(2):
                        acc[n][h] = acc[n][h] - below[n] * y[h]
        for n in range(2):
            for h in range(2):
                near[8 * n:8 * n + 8, 128 * h:128 * h + 128] = acc[n][h]
        inv[pl.ds(r0, NB), :] = jnp.where(lane - r0 <= sub, zb[...], 0.0)
        return carry

    for top in range(2):
        lax.fori_loop(top * STEPS // 2, (top + 1) * STEPS // 2, functools.partial(step, top=top), 0)


def kernel(flags, mine, other, panel, trail, trail_other, pf, up, nx, w, inv, *work):
    row, core = flags[0], flags[1]
    is0 = core == 0
    lane_all = lax.broadcasted_iota(jnp.int32, (N, N), 1)
    row_all = lax.broadcasted_iota(jnp.int32, (N, N), 0)
    low = lane_all <= row_all

    def pair(lo, hi):
        m, o = mine[:, lo:hi, :], other[:, lo:hi, :]
        return jnp.where(is0, m, o), jnp.where(is0, o, m)

    head = jnp.concatenate(pair(0, 8), 1).reshape(N, N)
    head = 0.5 * (head + head.T)
    w[...] = head
    factor_inverse(w, inv, *work)
    corner, block1 = [t.reshape(N, N) for t in pair(8, 24)]
    block2 = jnp.concatenate(pair(24, 32), 1).reshape(N, N)
    inv1 = inv[...]
    below1 = dot_nt(block1, inv1)
    corner = corner - dot_nt(below1, below1)
    corner = 0.5 * (corner + corner.T)
    w[...] = corner
    inv1 = split(inv1)
    below_own = split(jnp.where(is0, below1, dot_nt3(block2, inv1)))
    below1 = split(below1)
    for slot in range(2):
        rows = pl.ds(slot * N, N)
        solved = dot_nt3(panel[rows, :], inv1)
        carried = solved
        if slot == 0:
            first = row == 0
            solved = jnp.where(first & ~low, 0.0, solved)
            carried = jnp.where(first, 0.0, solved)
        pf[rows, :] = solved
        up[rows, :] = trail[rows, :] - dot_nt3(carried, below_own)
        lead = jnp.where(is0, trail[rows, :], trail_other[rows, :]) - dot_nt3(carried, below1)
        if slot == 0:
            lead = jnp.where(row == 1, corner, lead)
        trail_other[rows, :] = lead
    factor_inverse(w, inv, *work)
    half = split(inv[pl.ds(pl.multiple_of(core * 128, 128), 128), :])
    low_half = lane_all[:, :128] + core * 128 <= row_all[:, :128]
    for slot in range(2):
        rows = pl.ds(slot * N, N)
        solved = dot_nt3(trail_other[rows, :], half)
        if slot == 0:
            solved = jnp.where((row == 0) | ((row == 1) & ~low_half), 0.0, solved)
        nx[rows, :] = solved


def local_part(flags, mine, other, panel, trail, trail_other):
    vmem = pl.BlockSpec(memory_space=pltpu.VMEM)
    f32 = jnp.float32
    return pl.pallas_call(
        kernel,
        out_shape=[
            jax.ShapeDtypeStruct((512, N), f32),
            jax.ShapeDtypeStruct((512, N), f32),
            jax.ShapeDtypeStruct((512, 128), f32),
        ],
        in_specs=[pl.BlockSpec(memory_space=pltpu.SMEM)] + [vmem] * 5,
        out_specs=[vmem] * 3,
        scratch_shapes=[
            pltpu.VMEM((N, N), f32),
            pltpu.VMEM((N, N), f32),
            pltpu.VMEM((NB, N), f32),
            pltpu.VMEM((64, 128), f32),
            pltpu.VMEM((64, 128), f32),
            pltpu.VMEM((64, 128), f32),
            pltpu.VMEM((NB, N), f32),
            pltpu.VMEM((NB, N), f32),
            pltpu.VMEM((N, NB), f32),
        ],
        compiler_params=pltpu.CompilerParams(vmem_limit_bytes=40 << 20),
        name="panel_step",
    )(flags, mine, other, panel, trail, trail_other)


def on_device(panel, trail):
    plane = ("y", "x")
    z = lax.axis_index("z")
    member = lax.axis_index(plane)
    core = lax.axis_index("core")
    row = z * lax.axis_size(plane) + member
    trail_other = lax.ppermute(trail.reshape(512, N), "core", [(0, 1), (1, 0)])
    sent = jnp.where((row == 1) & (core == 0), trail[0, :, 0, :], panel[0]).reshape(16, 16, N)
    got = lax.all_to_all(sent, plane, 0, 0)
    shares = jnp.where(core == 0, got[:3:2, :8], got[:3:2, 8:])
    piece = jnp.concatenate([shares[0], got[1], shares[1]], 0)
    piece = jnp.where(z == 0, piece, 0.0)
    for pairs in Z_STEPS:
        piece = piece + lax.ppermute(piece, "z", pairs)
    mine = lax.all_to_all(jnp.broadcast_to(piece[None], (16, 32, N)), plane, 0, 0)
    other = lax.ppermute(mine, "core", [(0, 1), (1, 0)])
    flags = jnp.stack([row, core]).astype(jnp.int32)
    pf, up, nx = local_part(
        flags, mine, other, panel.reshape(512, N), trail.reshape(512, N), trail_other
    )
    return pf.reshape(2, N, N), up.reshape(2, N, 1, N), nx.reshape(2, N, 128)


def solution(mesh):
    grid = Mesh(mesh.devices.reshape(8, 4, 4, 2), ("z", "y", "x", "core"))
    rows = ("z", "y", "x")
    return jax.shard_map(
        on_device,
        mesh=grid,
        in_specs=(P(None, rows, None), P(None, rows, None, "core")),
        out_specs=(P(None, rows, None), P(None, rows, None, "core"), P(None, rows, "core")),
        check_vma=False,
    )
```

```python
import functools

import jax
import jax.numpy as jnp
from jax import lax
from jax.experimental import pallas as pl
from jax.experimental.pallas import tpu as pltpu
from jax.sharding import Mesh, PartitionSpec as P

N = 256
NB = 16
STEPS = N // NB
Z_STEPS = (
    [(0, 1)],
    [(0, 7), (1, 2)],
    [(0, 5), (1, 4), (2, 3), (7, 6)],
)


def dot_nt(a, b):
    return lax.dot_general(
        a, b, (((1,), (1,)), ((), ())),
        precision=lax.Precision.HIGHEST, preferred_element_type=jnp.float32,
    )


def split(a):
    high = a.astype(jnp.bfloat16)
    return high, (a - high.astype(jnp.float32)).astype(jnp.bfloat16)


def dot_nt3(a, b):
    a_hi, a_lo = split(a)
    b_hi, b_lo = b
    return lax.dot_general(
        jnp.concatenate([a_hi, a_hi, a_lo], 1), jnp.concatenate([b_hi, b_lo, b_hi], 1),
        (((1,), (1,)), ((), ())), preferred_element_type=jnp.float32,
    )


def three_parts(a):
    one = a.astype(jnp.bfloat16).astype(jnp.float32)
    two = (a - one).astype(jnp.bfloat16).astype(jnp.float32)
    return one, two, a - one - two


def dot_bf16(a, b):
    return lax.dot_general(a, b, (((1,), (0,)), ((), ())), preferred_element_type=jnp.float32)


def spread_row(ref, i, h):
    return jnp.broadcast_to(ref[i:i + 1, 128 * h:128 * h + 128], (8, 128))


def factor_inverse(w, inv, near, spl, low, mid, xb, zb, tt):
    lane = lax.broadcasted_iota(jnp.int32, (NB, N), 1)
    sub = lax.broadcasted_iota(jnp.int32, (NB, N), 0)
    zb[...] = jnp.zeros((NB, N), jnp.float32)
    near[...] = w[0:NB, :]

    def step(b, carry, top):
        r0 = pl.multiple_of(b * NB, NB)
        n0 = pl.multiple_of(jnp.minimum(r0 + NB, N - NB), NB)
        lo = 128 * top
        base = r0 - lo
        rows = near[...]
        half = rows[:, lo:lo + 128]

        def column(tile, j):
            idx = jnp.full((8, 128), base + j, jnp.int32)
            return jnp.take_along_axis(tile, idx, axis=1)

        for j in range(8):
            spl[8 * j:8 * j + 8, :] = column(half[:8], j)
        v = [[column(half[8:], j)] for j in range(8)]
        d = [column(half[8:], 8 + j) for j in range(8)]
        in_block = (lane >= r0) & (lane < r0 + NB)
        xb[...] = jnp.where(in_block, jnp.where(lane - r0 == sub, 1.0, 0.0), rows)
        z_old = zb[...]
        one, two, three = three_parts(z_old)
        left = jnp.concatenate([one, one, two, one, two, three], 0)
        right = jnp.concatenate([one, two, one, three, two, one], 0).astype(jnp.bfloat16)
        tt[lo:, :] = left[:, lo:].T.astype(jnp.bfloat16)
        gone = (lane >= r0 - NB) & (lane < r0)
        nxt = jnp.where(gone, 0.0, w[pl.ds(n0, NB), :]) - dot_bf16(tt[pl.ds(n0, NB), :], right)
        for j in range(8):
            v[j] += [column(nxt[:8, lo:lo + 128], j), column(nxt[8:, lo:lo + 128], j)]
        c = [[column(nxt[8 * n:8 * n + 8, lo:lo + 128], 8 + j) for n in range(2)] for j in range(8)]
        nxt = jnp.where(in_block, 0.0, nxt)
        acc = [[nxt[8 * n:8 * n + 8, 128 * h:128 * h + 128] for h in range(2)] for n in range(2)]
        lane_r = lax.broadcasted_iota(jnp.int32, (N - lo, N), 1)
        gone_r = (lane_r >= r0 - NB) & (lane_r < r0)
        w[lo:, :] = jnp.where(gone_r, 0.0, w[lo:, :]) - dot_bf16(tt[lo:, :], right)
        y_all = []
        for g in range(2):
            if g == 0:
                s = [[spread_row(spl, 8 * j + i, 0) for j in range(i + 1)] for i in range(8)]
            else:
                for j in range(8):
                    mid[8 * j:8 * j + 8, :] = d[j]
                s = [[spread_row(mid, 8 * j + i, 0) for j in range(i + 1)] for i in range(8)]
                v = c
            x = [[spread_row(xb, 8 * g + i, h) for h in range(2)] for i in range(8)]
            if g == 1:
                for k in range(8):
                    for i in range(8):
                        for h in range(2):
                            x[i][h] = x[i][h] - cross[k][i] * y_all[k][h]
            cross = []
            for k in range(8):
                r = lax.rsqrt(s[k][k])
                y = [x[k][h] * r for h in range(2)]
                y_all.append(y)
                for h in range(2):
                    zb[8 * g + k:8 * g + k + 1, 128 * h:128 * h + 128] = y[h][:1]
                col = [None] * 8
                for i in range(k + 1, 8):
                    col[i] = s[i][k] * r
                    for j in range(k + 1, i + 1):
                        s[i][j] = s[i][j] - col[i] * col[j]
                    for h in range(2):
                        x[i][h] = x[i][h] - col[i] * y[h]
                v[k] = [t * r for t in v[k]]
                for j in range(k + 1, 8):
                    v[j] = [t - u * col[j] for t, u in zip(v[j], v[k])]
                below = v[k]
                if g == 0:
                    low[8 * k:8 * k + 8, :] = v[k][0]
                    cross.append([spread_row(low, 8 * k + i, 0) for i in range(8)])
                    below = v[k][1:]
                    for j in range(8):
                        d[j] = d[j] - v[k][0] * cross[k][j]
                        c[j] = [t - u * cross[k][j] for t, u in zip(c[j], below)]
                for n in range(2):
                    for h in range(2):
                        acc[n][h] = acc[n][h] - below[n] * y[h]
        for n in range(2):
            for h in range(2):
                near[8 * n:8 * n + 8, 128 * h:128 * h + 128] = acc[n][h]
        inv[pl.ds(r0, NB), :] = jnp.where(lane - r0 <= sub, zb[...], 0.0)
        return carry

    for top in range(2):
        lax.fori_loop(top * STEPS // 2, (top + 1) * STEPS // 2, functools.partial(step, top=top), 0)


def kernel(flags, mine, other, panel, trail, trail_other, pf, up, nx, w, inv, *work):
    *work, panel_in, solved_out, up_out, nx_out, sems = work
    fetch = pltpu.make_async_copy(panel, panel_in, sems.at[0])
    fetch.start()
    row, core = flags[0], flags[1]
    is0 = core == 0
    lane_all = lax.broadcasted_iota(jnp.int32, (N, N), 1)
    row_all = lax.broadcasted_iota(jnp.int32, (N, N), 0)
    low = lane_all <= row_all

    def pair(lo, hi):
        m, o = mine[:, lo:hi, :], other[:, lo:hi, :]
        return jnp.where(is0, m, o), jnp.where(is0, o, m)

    head = jnp.concatenate(pair(0, 8), 1).reshape(N, N)
    head = 0.5 * (head + head.T)
    w[...] = head
    factor_inverse(w, inv, *work)
    corner, block1 = [t.reshape(N, N) for t in pair(8, 24)]
    block2 = jnp.concatenate(pair(24, 32), 1).reshape(N, N)
    inv1 = inv[...]
    below1 = dot_nt(block1, inv1)
    corner = corner - dot_nt(below1, below1)
    corner = 0.5 * (corner + corner.T)
    w[...] = corner
    inv1 = split(inv1)
    below_own = split(jnp.where(is0, below1, dot_nt3(block2, inv1)))
    below1 = split(below1)
    fetch.wait()
    copies = []
    for slot in range(2):
        rows = pl.ds(slot * N, N)
        solved = dot_nt3(panel_in[rows, :], inv1)
        carried = solved
        if slot == 0:
            first = row == 0
            solved = jnp.where(first & ~low, 0.0, solved)
            carried = jnp.where(first, 0.0, solved)
        solved_out[rows, :] = solved
        base = trail[rows, :]
        updated = base - dot_nt3(carried, below_own)
        for h in range(2):
            up_out[pl.ds(512 * slot + h, N, stride=2), :] = updated[:, 128 * h:128 * h + 128]
        lead = jnp.where(is0, base, trail_other[rows, :]) - dot_nt3(carried, below1)
        if slot == 0:
            lead = jnp.where(row == 1, corner, lead)
        trail_other[rows, :] = lead
    copies.append(pltpu.make_async_copy(solved_out, pf, sems.at[1]))
    copies.append(pltpu.make_async_copy(up_out, up, sems.at[2]))
    for copy in copies:
        copy.start()
    factor_inverse(w, inv, *work)
    half = split(inv[pl.ds(pl.multiple_of(core * 128, 128), 128), :])
    low_half = lane_all[:, :128] + core * 128 <= row_all[:, :128]
    for slot in range(2):
        rows = pl.ds(slot * N, N)
        solved = dot_nt3(trail_other[rows, :], half)
        if slot == 0:
            solved = jnp.where((row == 0) | ((row == 1) & ~low_half), 0.0, solved)
        nx_out[rows, :] = solved
        copy = pltpu.make_async_copy(nx_out.at[rows, :], nx.at[rows, :], sems.at[3 + slot])
        copy.start()
        copies.append(copy)
    for copy in copies:
        copy.wait()


def local_part(flags, mine, other, panel, trail, trail_other):
    vmem = pl.BlockSpec(memory_space=pltpu.VMEM)
    anywhere = pl.BlockSpec(memory_space=pl.ANY)
    f32 = jnp.float32
    return pl.pallas_call(
        kernel,
        out_shape=[
            jax.ShapeDtypeStruct((512, N), f32),
            jax.ShapeDtypeStruct((1024, 128), f32),
            jax.ShapeDtypeStruct((512, 128), f32),
        ],
        in_specs=[pl.BlockSpec(memory_space=pltpu.SMEM), vmem, vmem, anywhere, vmem, vmem],
        out_specs=[anywhere] * 3,
        scratch_shapes=[
            pltpu.VMEM((N, N), f32),
            pltpu.VMEM((N, N), f32),
            pltpu.VMEM((NB, N), f32),
            pltpu.VMEM((64, 128), f32),
            pltpu.VMEM((64, 128), f32),
            pltpu.VMEM((64, 128), f32),
            pltpu.VMEM((NB, N), f32),
            pltpu.VMEM((NB, N), f32),
            pltpu.VMEM((N, 6 * NB), jnp.bfloat16),
            pltpu.VMEM((512, N), f32),
            pltpu.VMEM((512, N), f32),
            pltpu.VMEM((1024, 128), f32),
            pltpu.VMEM((512, 128), f32),
            pltpu.SemaphoreType.DMA((5,)),
        ],
        compiler_params=pltpu.CompilerParams(vmem_limit_bytes=40 << 20),
        name="panel_step",
    )(flags, mine, other, panel, trail, trail_other)


def on_device(panel, trail):
    plane = ("y", "x")
    z = lax.axis_index("z")
    member = lax.axis_index(plane)
    core = lax.axis_index("core")
    row = z * lax.axis_size(plane) + member
    trail_other = lax.ppermute(trail.reshape(512, N), "core", [(0, 1), (1, 0)])
    sent = jnp.where((row == 1) & (core == 0), trail[0, :, 0, :], panel[0]).reshape(16, 16, N)
    got = lax.all_to_all(sent, plane, 0, 0)
    shares = jnp.where(core == 0, got[:3:2, :8], got[:3:2, 8:])
    piece = jnp.concatenate([shares[0], got[1], shares[1]], 0)
    piece = jnp.where(z == 0, piece, 0.0)
    for pairs in Z_STEPS:
        piece = piece + lax.ppermute(piece, "z", pairs)
    mine = lax.all_to_all(jnp.broadcast_to(piece[None], (16, 32, N)), plane, 0, 0)
    other = lax.ppermute(mine, "core", [(0, 1), (1, 0)])
    flags = jnp.stack([row, core]).astype(jnp.int32)
    pf, up, nx = local_part(
        flags, mine, other, panel.reshape(512, N), trail.reshape(512, N), trail_other
    )
    return pf.reshape(2, N, N), up.reshape(2, N, 1, N), nx.reshape(2, N, 128)


def solution(mesh):
    grid = Mesh(mesh.devices.reshape(8, 4, 4, 2), ("z", "y", "x", "core"))
    rows = ("z", "y", "x")
    return jax.shard_map(
        on_device,
        mesh=grid,
        in_specs=(P(None, rows, None), P(None, rows, None, "core")),
        out_specs=(P(None, rows, None), P(None, rows, None, "core"), P(None, rows, "core")),
        check_vma=False,
    )
```

```python
import functools

import jax
import jax.numpy as jnp
from jax import lax
from jax.experimental import pallas as pl
from jax.experimental.pallas import tpu as pltpu
from jax.sharding import Mesh, PartitionSpec as P

N = 256
NB = 16
STEPS = N // NB
Z_STEPS = (
    [(0, 1)],
    [(0, 7), (1, 2)],
    [(0, 5), (1, 4), (2, 3), (7, 6)],
)


def split(a):
    high = a.astype(jnp.bfloat16)
    return high, (a - high.astype(jnp.float32)).astype(jnp.bfloat16)


def dot_nt3(a, b):
    a_hi, a_lo = split(a)
    b_hi, b_lo = b
    return lax.dot_general(
        jnp.concatenate([a_hi, a_hi, a_lo], 1), jnp.concatenate([b_hi, b_lo, b_hi], 1),
        (((1,), (1,)), ((), ())), preferred_element_type=jnp.float32,
    )


def three_parts(a):
    one = a.astype(jnp.bfloat16).astype(jnp.float32)
    two = (a - one).astype(jnp.bfloat16).astype(jnp.float32)
    return one, two, a - one - two


def stack_six(a, b):
    a1, a2, a3 = [t.astype(jnp.bfloat16) for t in three_parts(a)]
    b1, b2, b3 = [t.astype(jnp.bfloat16) for t in three_parts(b)]
    return jnp.concatenate([a1, a1, a2, a1, a2, a3], 1), jnp.concatenate([b1, b2, b1, b3, b2, b1], 1)


def dot_nt6(a, b):
    a, b = stack_six(a, b)
    return lax.dot_general(a, b, (((1,), (1,)), ((), ())), preferred_element_type=jnp.float32)


def dot_bf16(a, b):
    return lax.dot_general(a, b, (((1,), (0,)), ((), ())), preferred_element_type=jnp.float32)


def spread_row(ref, i, h):
    return jnp.broadcast_to(ref[i:i + 1, 128 * h:128 * h + 128], (8, 128))


def factor_inverse(w, inv, near, spl, low, mid, xb, zb, tt):
    lane = lax.broadcasted_iota(jnp.int32, (NB, N), 1)
    sub = lax.broadcasted_iota(jnp.int32, (NB, N), 0)
    zb[...] = jnp.zeros((NB, N), jnp.float32)
    near[...] = w[0:NB, :]

    def step(b, carry, top):
        r0 = pl.multiple_of(b * NB, NB)
        n0 = pl.multiple_of(jnp.minimum(r0 + NB, N - NB), NB)
        lo = 128 * top
        base = r0 - lo
        rows = near[...]
        half = rows[:, lo:lo + 128]

        def column(tile, j):
            idx = jnp.full((8, 128), base + j, jnp.int32)
            return jnp.take_along_axis(tile, idx, axis=1)

        for j in range(8):
            spl[8 * j:8 * j + 8, :] = column(half[:8], j)
        v = [[column(half[8:], j)] for j in range(8)]
        d = [column(half[8:], 8 + j) for j in range(8)]
        in_block = (lane >= r0) & (lane < r0 + NB)
        xb[...] = jnp.where(in_block, jnp.where(lane - r0 == sub, 1.0, 0.0), rows)
        z_old = zb[...]
        one, two, three = three_parts(z_old)
        left = jnp.concatenate([one, one, two, one, two, three], 0)
        right = jnp.concatenate([one, two, one, three, two, one], 0).astype(jnp.bfloat16)
        tt[lo:, :] = left[:, lo:].T.astype(jnp.bfloat16)
        gone = (lane >= r0 - NB) & (lane < r0)
        nxt = jnp.where(gone, 0.0, w[pl.ds(n0, NB), :]) - dot_bf16(tt[pl.ds(n0, NB), :], right)
        for j in range(8):
            v[j] += [column(nxt[:8, lo:lo + 128], j), column(nxt[8:, lo:lo + 128], j)]
        c = [[column(nxt[8 * n:8 * n + 8, lo:lo + 128], 8 + j) for n in range(2)] for j in range(8)]
        nxt = jnp.where(in_block, 0.0, nxt)
        acc = [[nxt[8 * n:8 * n + 8, 128 * h:128 * h + 128] for h in range(2)] for n in range(2)]
        lane_r = lax.broadcasted_iota(jnp.int32, (N - lo, 128), 1) + lo
        gone_r = (lane_r >= r0 - NB) & (lane_r < r0)
        late = dot_bf16(tt[lo:, :], right)
        w[lo:, lo:lo + 128] = jnp.where(gone_r, 0.0, w[lo:, lo:lo + 128]) - late[:, lo:lo + 128]
        w[lo:, 128 - lo:256 - lo] = w[lo:, 128 - lo:256 - lo] - late[:, 128 - lo:256 - lo]
        x_low = [xb[8:, 128 * h:128 * h + 128] for h in range(2)]
        for g in range(2):
            if g == 0:
                s = [[spread_row(spl, 8 * j + i, 0) for j in range(i + 1)] for i in range(8)]
            else:
                for j in range(8):
                    mid[8 * j:8 * j + 8, :] = d[j]
                s = [[spread_row(mid, 8 * j + i, 0) for j in range(i + 1)] for i in range(8)]
                v = c
                for h in range(2):
                    xb[8:, 128 * h:128 * h + 128] = x_low[h]
            x = [[spread_row(xb, 8 * g + i, h) for h in range(2)] for i in range(8)]
            cross = []
            for k in range(8):
                r = lax.rsqrt(s[k][k])
                y = [x[k][h] * r for h in range(2)]
                for h in range(2):
                    zb[8 * g + k:8 * g + k + 1, 128 * h:128 * h + 128] = y[h][:1]
                col = [None] * 8
                for i in range(k + 1, 8):
                    col[i] = s[i][k] * r
                    for j in range(k + 1, i + 1):
                        s[i][j] = s[i][j] - col[i] * col[j]
                    for h in range(2):
                        x[i][h] = x[i][h] - col[i] * y[h]
                v[k] = [t * r for t in v[k]]
                for j in range(k + 1, 8):
                    v[j] = [t - u * col[j] for t, u in zip(v[j], v[k])]
                below = v[k]
                if g == 0:
                    low[8 * k:8 * k + 8, :] = v[k][0]
                    cross.append([spread_row(low, 8 * k + i, 0) for i in range(8)])
                    below = v[k][1:]
                    x_low = [t - v[k][0] * u for t, u in zip(x_low, y)]
                    for j in range(8):
                        d[j] = d[j] - v[k][0] * cross[k][j]
                        c[j] = [t - u * cross[k][j] for t, u in zip(c[j], below)]
                for n in range(2):
                    for h in range(2):
                        acc[n][h] = acc[n][h] - below[n] * y[h]
        for n in range(2):
            for h in range(2):
                near[8 * n:8 * n + 8, 128 * h:128 * h + 128] = acc[n][h]
        inv[pl.ds(r0, NB), :] = jnp.where(lane - r0 <= sub, zb[...], 0.0)
        return carry

    for top in range(2):
        lax.fori_loop(top * STEPS // 4, (top + 1) * STEPS // 4, lambda t, c: step(2 * t + 1, step(2 * t, c, top), top), 0)
        if top == 0:
            kept = lax.broadcasted_iota(jnp.int32, (128, 128), 1) < 128 - NB
            w[128:, :128] = jnp.where(kept, w[128:, :128], 0.0)


def kernel(flags, mine, other, panel, trail, trail_other, pf, up, nx, w, inv, *work):
    *work, panel_in, solved_out, up_out, nx_out, sems = work
    fetch = pltpu.make_async_copy(panel, panel_in, sems.at[0])
    fetch.start()
    row, core = flags[0], flags[1]
    is0 = core == 0
    lane_all = lax.broadcasted_iota(jnp.int32, (N, N), 1)
    row_all = lax.broadcasted_iota(jnp.int32, (N, N), 0)
    low = lane_all <= row_all

    def pair(lo, hi):
        m, o = mine[:, lo:hi, :], other[:, lo:hi, :]
        return jnp.where(is0, m, o), jnp.where(is0, o, m)

    head = jnp.concatenate(pair(0, 8), 1).reshape(N, N)
    head = 0.5 * (head + head.T)
    w[...] = head
    factor_inverse(w, inv, *work)
    corner, block1 = [t.reshape(N, N) for t in pair(8, 24)]
    block2 = jnp.concatenate(pair(24, 32), 1).reshape(N, N)
    inv1 = inv[...]
    below1 = dot_nt6(block1, inv1)
    corner = 0.5 * (corner + corner.T) - dot_nt6(below1, below1)
    w[...] = corner
    inv1 = split(inv1)
    below_own = split(jnp.where(is0, below1, dot_nt3(block2, inv1)))
    below1 = split(below1)
    fetch.wait()
    copies = []
    for slot in range(2):
        rows = pl.ds(slot * N, N)
        solved = dot_nt3(panel_in[rows, :], inv1)
        carried = solved
        if slot == 0:
            first = row == 0
            solved = jnp.where(first & ~low, 0.0, solved)
            carried = jnp.where(first, 0.0, solved)
        solved_out[rows, :] = solved
        base = trail[rows, :]
        updated = base - dot_nt3(carried, below_own)
        for h in range(2):
            up_out[pl.ds(512 * slot + h, N, stride=2), :] = updated[:, 128 * h:128 * h + 128]
        lead = jnp.where(is0, base, trail_other[rows, :]) - dot_nt3(carried, below1)
        if slot == 0:
            lead = jnp.where(row == 1, corner, lead)
        trail_other[rows, :] = lead
    copies.append(pltpu.make_async_copy(solved_out, pf, sems.at[1]))
    copies.append(pltpu.make_async_copy(up_out, up, sems.at[2]))
    for copy in copies:
        copy.start()
    factor_inverse(w, inv, *work)
    half = split(inv[pl.ds(pl.multiple_of(core * 128, 128), 128), :])
    low_half = lane_all[:, :128] + core * 128 <= row_all[:, :128]
    for slot in range(2):
        rows = pl.ds(slot * N, N)
        solved = dot_nt3(trail_other[rows, :], half)
        if slot == 0:
            solved = jnp.where((row == 0) | ((row == 1) & ~low_half), 0.0, solved)
        nx_out[rows, :] = solved
        copy = pltpu.make_async_copy(nx_out.at[rows, :], nx.at[rows, :], sems.at[3 + slot])
        copy.start()
        copies.append(copy)
    for copy in copies:
        copy.wait()


def local_part(flags, mine, other, panel, trail, trail_other):
    vmem = pl.BlockSpec(memory_space=pltpu.VMEM)
    anywhere = pl.BlockSpec(memory_space=pl.ANY)
    f32 = jnp.float32
    return pl.pallas_call(
        kernel,
        out_shape=[
            jax.ShapeDtypeStruct((512, N), f32),
            jax.ShapeDtypeStruct((1024, 128), f32),
            jax.ShapeDtypeStruct((512, 128), f32),
        ],
        in_specs=[pl.BlockSpec(memory_space=pltpu.SMEM), vmem, vmem, anywhere, vmem, vmem],
        out_specs=[anywhere] * 3,
        scratch_shapes=[
            pltpu.VMEM((N, N), f32),
            pltpu.VMEM((N, N), f32),
            pltpu.VMEM((NB, N), f32),
            pltpu.VMEM((64, 128), f32),
            pltpu.VMEM((64, 128), f32),
            pltpu.VMEM((64, 128), f32),
            pltpu.VMEM((NB, N), f32),
            pltpu.VMEM((NB, N), f32),
            pltpu.VMEM((N, 6 * NB), jnp.bfloat16),
            pltpu.VMEM((512, N), f32),
            pltpu.VMEM((512, N), f32),
            pltpu.VMEM((1024, 128), f32),
            pltpu.VMEM((512, 128), f32),
            pltpu.SemaphoreType.DMA((5,)),
        ],
        compiler_params=pltpu.CompilerParams(vmem_limit_bytes=40 << 20),
        name="panel_step",
    )(flags, mine, other, panel, trail, trail_other)


def on_device(panel, trail):
    plane = ("y", "x")
    z = lax.axis_index("z")
    member = lax.axis_index(plane)
    core = lax.axis_index("core")
    row = z * lax.axis_size(plane) + member
    trail_other = lax.ppermute(trail.reshape(512, N), "core", [(0, 1), (1, 0)])
    sent = jnp.where((row == 1) & (core == 0), trail[0, :, 0, :], panel[0]).reshape(16, 16, N)
    got = lax.all_to_all(sent, plane, 0, 0)
    shares = jnp.where(core == 0, got[:3:2, :8], got[:3:2, 8:])
    piece = jnp.concatenate([shares[0], got[1], shares[1]], 0)
    piece = jnp.where(z == 0, piece, 0.0)
    for pairs in Z_STEPS:
        piece = piece + lax.ppermute(piece, "z", pairs)
    mine = lax.all_to_all(jnp.broadcast_to(piece[None], (16, 32, N)), plane, 0, 0)
    other = lax.ppermute(mine, "core", [(0, 1), (1, 0)])
    flags = jnp.stack([row, core]).astype(jnp.int32)
    pf, up, nx = local_part(
        flags, mine, other, panel.reshape(512, N), trail.reshape(512, N), trail_other
    )
    return pf.reshape(2, N, N), up.reshape(2, N, 1, N), nx.reshape(2, N, 128)


def solution(mesh):
    grid = Mesh(mesh.devices.reshape(8, 4, 4, 2), ("z", "y", "x", "core"))
    rows = ("z", "y", "x")
    return jax.shard_map(
        on_device,
        mesh=grid,
        in_specs=(P(None, rows, None), P(None, rows, None, "core")),
        out_specs=(P(None, rows, None), P(None, rows, None, "core"), P(None, rows, "core")),
        check_vma=False,
    )
```

```python
import functools

import jax
import jax.numpy as jnp
from jax import lax
from jax.experimental import pallas as pl
from jax.experimental.pallas import tpu as pltpu
from jax.sharding import Mesh, PartitionSpec as P

N = 256
NB = 16
STEPS = N // NB
Z_STEPS = (
    [(0, 1)],
    [(0, 7), (1, 2)],
    [(0, 5), (1, 4), (2, 3), (7, 6)],
)


def split(a):
    high = a.astype(jnp.bfloat16)
    return high, (a - high.astype(jnp.float32)).astype(jnp.bfloat16)


def dot_nt3(a, b):
    a_hi, a_lo = split(a)
    b_hi, b_lo = b
    return lax.dot_general(
        jnp.concatenate([a_hi, a_hi, a_lo], 1), jnp.concatenate([b_hi, b_lo, b_hi], 1),
        (((1,), (1,)), ((), ())), preferred_element_type=jnp.float32,
    )


def three_parts(a):
    one = a.astype(jnp.bfloat16).astype(jnp.float32)
    two = (a - one).astype(jnp.bfloat16).astype(jnp.float32)
    return one, two, a - one - two


def stack_six(a, b):
    a1, a2, a3 = [t.astype(jnp.bfloat16) for t in three_parts(a)]
    b1, b2, b3 = [t.astype(jnp.bfloat16) for t in three_parts(b)]
    return jnp.concatenate([a1, a1, a2, a1, a2, a3], 1), jnp.concatenate([b1, b2, b1, b3, b2, b1], 1)


def dot_nt6(a, b):
    a, b = stack_six(a, b)
    return lax.dot_general(a, b, (((1,), (1,)), ((), ())), preferred_element_type=jnp.float32)


def dot_bf16(a, b):
    return lax.dot_general(a, b, (((1,), (0,)), ((), ())), preferred_element_type=jnp.float32)


def spread_row(ref, i, h):
    return jnp.broadcast_to(ref[i:i + 1, 128 * h:128 * h + 128], (8, 128))


def factor_inverse(w, inv, near, spl, low, mid, xb, zb, tt):
    lane = lax.broadcasted_iota(jnp.int32, (NB, N), 1)
    sub = lax.broadcasted_iota(jnp.int32, (NB, N), 0)
    zb[...] = jnp.zeros((NB, N), jnp.float32)
    near[...] = w[0:NB, :]

    def step(b, carry, top):
        r0 = pl.multiple_of(b * NB, NB)
        n0 = pl.multiple_of(jnp.minimum(r0 + NB, N - NB), NB)
        lo = 128 * top
        base = r0 - lo
        rows = near[...]
        half = rows[:, lo:lo + 128]

        def column(tile, j):
            idx = jnp.full((8, 128), base + j, jnp.int32)
            return jnp.take_along_axis(tile, idx, axis=1)

        for j in range(8):
            spl[8 * j:8 * j + 8, :] = column(half[:8], j)
        v = [[column(half[8:], j)] for j in range(8)]
        d = [column(half[8:], 8 + j) for j in range(8)]
        in_block = (lane >= r0) & (lane < r0 + NB)
        xb[...] = jnp.where(in_block, jnp.where(lane - r0 == sub, 1.0, 0.0), rows)
        z_old = zb[...]
        one, two, three = three_parts(z_old)
        left = jnp.concatenate([one, one, two, one, two, three], 0)
        right = jnp.concatenate([one, two, one, three, two, one], 0).astype(jnp.bfloat16)
        tt[lo:, :] = left[:, lo:].T.astype(jnp.bfloat16)
        gone = (lane >= r0 - NB) & (lane < r0)
        nxt = jnp.where(gone, 0.0, w[pl.ds(n0, NB), :]) - dot_bf16(tt[pl.ds(n0, NB), :], right)
        for j in range(8):
            v[j] += [column(nxt[:8, lo:lo + 128], j), column(nxt[8:, lo:lo + 128], j)]
        c = [[column(nxt[8 * n:8 * n + 8, lo:lo + 128], 8 + j) for n in range(2)] for j in range(8)]
        nxt = jnp.where(in_block, 0.0, nxt)
        acc = [[nxt[8 * n:8 * n + 8, 128 * h:128 * h + 128] for h in range(2)] for n in range(2)]
        lane_r = lax.broadcasted_iota(jnp.int32, (N - lo, 128), 1) + lo
        gone_r = (lane_r >= r0 - NB) & (lane_r < r0)
        late = dot_bf16(tt[lo:, :], right)
        w[lo:, lo:lo + 128] = jnp.where(gone_r, 0.0, w[lo:, lo:lo + 128]) - late[:, lo:lo + 128]
        w[lo:, 128 - lo:256 - lo] = w[lo:, 128 - lo:256 - lo] - late[:, 128 - lo:256 - lo]
        x_low = [xb[8:, 128 * h:128 * h + 128] for h in range(2)]
        for g in range(2):
            if g == 0:
                s = [[spread_row(spl, 8 * j + i, 0) for j in range(i + 1)] for i in range(8)]
            else:
                for j in range(8):
                    mid[8 * j:8 * j + 8, :] = d[j]
                s = [[spread_row(mid, 8 * j + i, 0) for j in range(i + 1)] for i in range(8)]
                v = c
                for h in range(2):
                    xb[8:, 128 * h:128 * h + 128] = x_low[h]
            x = [[spread_row(xb, 8 * g + i, h) for h in range(2)] for i in range(8)]
            cross = []
            for k in range(8):
                r = lax.rsqrt(s[k][k])
                y = [x[k][h] * r for h in range(2)]
                for h in range(2):
                    zb[8 * g + k:8 * g + k + 1, 128 * h:128 * h + 128] = y[h][:1]
                col = [None] * 8
                for i in range(k + 1, 8):
                    col[i] = s[i][k] * r
                    for j in range(k + 1, i + 1):
                        s[i][j] = s[i][j] - col[i] * col[j]
                    for h in range(2):
                        x[i][h] = x[i][h] - col[i] * y[h]
                v[k] = [t * r for t in v[k]]
                for j in range(k + 1, 8):
                    v[j] = [t - u * col[j] for t, u in zip(v[j], v[k])]
                below = v[k]
                if g == 0:
                    low[8 * k:8 * k + 8, :] = v[k][0]
                    cross.append([spread_row(low, 8 * k + i, 0) for i in range(8)])
                    below = v[k][1:]
                    x_low = [t - v[k][0] * u for t, u in zip(x_low, y)]
                    for j in range(8):
                        d[j] = d[j] - v[k][0] * cross[k][j]
                        c[j] = [t - u * cross[k][j] for t, u in zip(c[j], below)]
                for n in range(2):
                    for h in range(2):
                        acc[n][h] = acc[n][h] - below[n] * y[h]
        for n in range(2):
            for h in range(2):
                near[8 * n:8 * n + 8, 128 * h:128 * h + 128] = acc[n][h]
        inv[pl.ds(r0, NB), :] = jnp.where(lane - r0 <= sub, zb[...], 0.0)
        return carry

    for top in range(2):
        lax.fori_loop(top * STEPS // 4, (top + 1) * STEPS // 4, lambda t, c: step(2 * t + 1, step(2 * t, c, top), top), 0)
        if top == 0:
            kept = lax.broadcasted_iota(jnp.int32, (128, 128), 1) < 128 - NB
            w[128:, :128] = jnp.where(kept, w[128:, :128], 0.0)


def lead_kernel(blocks, inv, w, *work):
    head = blocks[:, :16, :].reshape(N, N)
    w[...] = 0.5 * (head + head.T)
    factor_inverse(w, inv, *work)


def kernel(flags, blocks, swapped, inv_lead, panel, trail, trail_other, pf, up, nx, w, inv, *work):
    row, core = flags[0], flags[1]
    is0 = core == 0
    lane_all = lax.broadcasted_iota(jnp.int32, (N, N), 1)
    row_all = lax.broadcasted_iota(jnp.int32, (N, N), 0)
    low = lane_all <= row_all
    *work, panel_in, solved_out, up_out, nx_out, sems = work
    fetch = pltpu.make_async_copy(panel, panel_in, sems.at[0])
    fetch.start()
    held, missing = blocks[:, 16:32, :].reshape(N, N), swapped[:, :16, :].reshape(N, N)
    corner, block1 = jnp.where(is0, held, missing), jnp.where(is0, missing, held)
    part, rest = blocks[:, 32:, :], swapped[:, 16:, :]
    block2 = jnp.concatenate([jnp.where(is0, part, rest), jnp.where(is0, rest, part)], 1).reshape(N, N)
    inv1 = inv_lead[...]
    below1 = dot_nt6(block1, inv1)
    corner = 0.5 * (corner + corner.T) - dot_nt6(below1, below1)
    w[...] = corner
    inv1 = split(inv1)
    below_own = split(jnp.where(is0, below1, dot_nt3(block2, inv1)))
    below1 = split(below1)
    fetch.wait()
    copies = []
    for slot in range(2):
        rows = pl.ds(slot * N, N)
        solved = dot_nt3(panel_in[rows, :], inv1)
        carried = solved
        if slot == 0:
            first = row == 0
            solved = jnp.where(first & ~low, 0.0, solved)
            carried = jnp.where(first, 0.0, solved)
        solved_out[rows, :] = solved
        base = trail[rows, :]
        updated = base - dot_nt3(carried, below_own)
        for h in range(2):
            up_out[pl.ds(512 * slot + h, N, stride=2), :] = updated[:, 128 * h:128 * h + 128]
        lead = jnp.where(is0, base, trail_other[rows, :]) - dot_nt3(carried, below1)
        if slot == 0:
            lead = jnp.where(row == 1, corner, lead)
        trail_other[rows, :] = lead
    copies.append(pltpu.make_async_copy(solved_out, pf, sems.at[1]))
    copies.append(pltpu.make_async_copy(up_out, up, sems.at[2]))
    for copy in copies:
        copy.start()
    factor_inverse(w, inv, *work)
    half = split(inv[pl.ds(pl.multiple_of(core * 128, 128), 128), :])
    low_half = lane_all[:, :128] + core * 128 <= row_all[:, :128]
    for slot in range(2):
        rows = pl.ds(slot * N, N)
        solved = dot_nt3(trail_other[rows, :], half)
        if slot == 0:
            solved = jnp.where((row == 0) | ((row == 1) & ~low_half), 0.0, solved)
        nx_out[rows, :] = solved
        copy = pltpu.make_async_copy(nx_out.at[rows, :], nx.at[rows, :], sems.at[3 + slot])
        copy.start()
        copies.append(copy)
    for copy in copies:
        copy.wait()


WORK = [
    pltpu.VMEM((N, N), jnp.float32),
    pltpu.VMEM((NB, N), jnp.float32),
    pltpu.VMEM((64, 128), jnp.float32),
    pltpu.VMEM((64, 128), jnp.float32),
    pltpu.VMEM((64, 128), jnp.float32),
    pltpu.VMEM((NB, N), jnp.float32),
    pltpu.VMEM((NB, N), jnp.float32),
    pltpu.VMEM((N, 6 * NB), jnp.bfloat16),
]


def factor_lead(blocks):
    vmem = pl.BlockSpec(memory_space=pltpu.VMEM)
    return pl.pallas_call(
        lead_kernel,
        out_shape=jax.ShapeDtypeStruct((N, N), jnp.float32),
        in_specs=[vmem],
        out_specs=vmem,
        scratch_shapes=WORK,
        compiler_params=pltpu.CompilerParams(vmem_limit_bytes=16 << 20),
        cost_estimate=pl.CostEstimate(flops=4 << 30, bytes_accessed=8 << 20, transcendentals=0),
        name="factor_lead",
    )(blocks)


def local_part(flags, blocks, swapped, inv_lead, panel, trail, trail_other):
    vmem = pl.BlockSpec(memory_space=pltpu.VMEM)
    anywhere = pl.BlockSpec(memory_space=pl.ANY)
    f32 = jnp.float32
    return pl.pallas_call(
        kernel,
        out_shape=[
            jax.ShapeDtypeStruct((512, N), f32),
            jax.ShapeDtypeStruct((1024, 128), f32),
            jax.ShapeDtypeStruct((512, 128), f32),
        ],
        in_specs=[pl.BlockSpec(memory_space=pltpu.SMEM), vmem, vmem, vmem, anywhere, vmem, vmem],
        out_specs=[anywhere] * 3,
        scratch_shapes=WORK[:1] + WORK + [
            pltpu.VMEM((512, N), f32),
            pltpu.VMEM((512, N), f32),
            pltpu.VMEM((1024, 128), f32),
            pltpu.VMEM((512, 128), f32),
            pltpu.SemaphoreType.DMA((5,)),
        ],
        compiler_params=pltpu.CompilerParams(vmem_limit_bytes=40 << 20),
        name="panel_step",
    )(flags, blocks, swapped, inv_lead, panel, trail, trail_other)


def on_device(panel, trail):
    plane = ("y", "x")
    z = lax.axis_index("z")
    member = lax.axis_index(plane)
    core = lax.axis_index("core")
    row = z * lax.axis_size(plane) + member
    trail_other = lax.ppermute(trail.reshape(512, N), "core", [(0, 1), (1, 0)])
    sent = jnp.where((row == 1) & (core == 0), trail[0, :, 0, :], panel[0]).reshape(16, 16, N)
    got = lax.all_to_all(sent, plane, 0, 0)
    share = jnp.where(core == 0, got[2, :8], got[2, 8:])
    piece = jnp.concatenate([got[0], got[1], share], 0)
    piece = jnp.where(z == 0, piece, 0.0)
    for pairs in Z_STEPS:
        piece = piece + lax.ppermute(piece, "z", pairs)
    blocks = lax.all_to_all(jnp.broadcast_to(piece[None], (16, 40, N)), plane, 0, 0)
    swapped = lax.ppermute(blocks[:, 16:], "core", [(0, 1), (1, 0)])
    inv_lead = factor_lead(blocks)
    flags = jnp.stack([row, core]).astype(jnp.int32)
    pf, up, nx = local_part(
        flags, blocks, swapped, inv_lead,
        panel.reshape(512, N), trail.reshape(512, N), trail_other,
    )
    return pf.reshape(2, N, N), up.reshape(2, N, 1, N), nx.reshape(2, N, 128)


def solution(mesh):
    grid = Mesh(mesh.devices.reshape(8, 4, 4, 2), ("z", "y", "x", "core"))
    rows = ("z", "y", "x")
    return jax.shard_map(
        on_device,
        mesh=grid,
        in_specs=(P(None, rows, None), P(None, rows, None, "core")),
        out_specs=(P(None, rows, None), P(None, rows, None, "core"), P(None, rows, "core")),
        check_vma=False,
    )
```
